256 devices in a mesh: cell: 32 (over y, z), lt: 8 (over x, core).
Axes of the slice: x: 4, y: 4, z: 8, core: 2. Of those that a mesh axis runs over, the one named last changes fastest.
Arguments:
- field: float32 [8, 80, 1048576], P('lt', None, 'cell'), may hold values from -54 to 54
- level_start: float32 [80, 24], replicated, may hold values from -6 to 6
- time_start: float32 [8, 6], replicated, may hold values from -6 to 6
Outputs:
- core: float32 [6, 24, 1048576], P(None, 'lt', 'cell')
- level_basis: float32 [80, 24], replicated
- time_basis: float32 [8, 6], replicated
The draws below stay inside these ranges and needn't reach their ends.
All inputs are finite; a program needn't handle non-finite values.
Results may differ from the reference program's by a relative error of at most 0.0003.
Values sent between devices are 32-bit elements; how exact they have to be, the bound alone decides.
No kernel may reach another device: no remote copies, remote signals or barrier semaphores. Data moves between devices by JAX's collectives and lax.ppermute only.
A program may use at most 64 MiB of HBM per device.

```python
import math
import jax
import jax.numpy as jnp
from jax import lax

LEV = 80
SNAP = 8
R1 = 24
R2 = 6
ITERS = 3
CELLS = 1048576


def draw_field(key, part):
    keys = jax.random.split(key, 5)
    mode_count = 12
    level_scale = jnp.exp(jax.random.uniform(keys[0], (LEV,), jnp.float32, 0.0, math.log(3.0)))
    base = jnp.clip(jax.random.normal(keys[1], (mode_count,), jnp.float32), -2.5, 2.5)
    wobble = jnp.clip(jax.random.normal(keys[2], (SNAP, mode_count), jnp.float32), -3.0, 3.0)
    cell_modes = jnp.clip(jax.random.normal(keys[3], (mode_count, CELLS), jnp.float32), -3.0, 3.0)
    noise = 0.6 * jnp.clip(jax.random.normal(keys[4], (SNAP, LEV, CELLS), jnp.float32), -4.0, 4.0)
    level_place = (jnp.arange(LEV).astype(jnp.float32) + 0.5) / LEV
    weights = base[None, :] + 0.5 * wobble
    signal = jnp.zeros((SNAP, LEV, CELLS), jnp.float32)
    for mode in range(mode_count):
        profile = jnp.cos(math.pi * (mode + 0.5) * level_place) * 0.85 ** mode
        signal = signal + 0.5 * weights[:, mode][:, None, None] * profile[None, :, None] * cell_modes[mode][None, None, :]
    position = jnp.arange(CELLS).astype(jnp.float32)
    rising = 1.0 + 2.0 * position / max(CELLS - 1, 1)
    total = (signal + noise) * level_scale[None, :, None] * rising[None, None, :]
    return jnp.clip(total, -54.0, 54.0)


def centred(own_key, shape, spread, most, held_as=jnp.bfloat16):
    return jnp.clip(spread * jax.random.normal(own_key, shape, jnp.float32), -most, most).astype(held_as)


def setup_inputs(seed: int = 0) -> dict:
    seeds = jax.random.split(jax.random.key(seed), 4)
    field = draw_field(jax.random.fold_in(seeds[3], 71), 0)
    level_start = centred(seeds[1], (LEV, R1), 1.0, 6.0, jnp.float32)
    time_start = centred(seeds[2], (SNAP, R2), 1.0, 6.0, jnp.float32)
    return dict(field=field, level_start=level_start, time_start=time_start)


highest = lax.Precision.HIGHEST

def orthonormal(matrix):
    square = jnp.dot(matrix.T, matrix, precision=highest)
    factor = jnp.linalg.cholesky(square)
    return lax.linalg.triangular_solve(factor, matrix, left_side=False, lower=True, transpose_a=True)

def subspace(gram, start):
    basis = orthonormal(start)
    for step in range(ITERS):
        basis = orthonormal(jnp.dot(gram, basis, precision=highest))
    return basis

def reference(field, level_start, time_start):
    level_gram = jnp.zeros((LEV, LEV), jnp.float32)
    for snapshot in range(SNAP):
        level_gram = level_gram + jnp.dot(field[snapshot], field[snapshot].T, precision=highest)
    level_basis = subspace(level_gram, level_start)
    reduced = jnp.einsum('lr,slc->src', level_basis, field, precision=highest)
    time_gram = jnp.einsum('src,trc->st', reduced, reduced, precision=highest)
    time_basis = subspace(time_gram, time_start)
    core = jnp.einsum('sq,src->qrc', time_basis, reduced, precision=highest)
    return (core, level_basis, time_basis)
```

```python
import jax
import jax.numpy as jnp
from jax import lax
from jax.experimental import pallas as pl
from jax.experimental.pallas import tpu as pltpu
from jax.sharding import PartitionSpec as P

ITERS = 3
highest = lax.Precision.HIGHEST
f32 = jnp.float32
bf16 = jnp.bfloat16
LEV, R1, SNAP, R2 = 80, 24, 8, 6
LANES = 128


def split(x, parts):
    out = []
    for _ in range(parts):
        top = x.astype(bf16)
        out.append(top)
        x = x - top.astype(f32)
    return out


def orth_rows(w, n):
    rows = w.shape[0]
    cols = [
        jnp.broadcast_to(jnp.sum(w * w[k : k + 1, :], axis=1, keepdims=True), w.shape)
        for k in range(n)
    ]
    row = lax.broadcasted_iota(jnp.int32, w.shape, 0)
    for k in range(n):
        pivot = cols[k][k : k + 1, :]
        inv = lax.rsqrt(pivot)
        inv = inv * (1.5 - (0.5 * pivot * inv) * inv)
        done = w[k : k + 1, :] * inv
        low = jnp.where(row > k, cols[k] * inv, 0.0)
        w = jnp.where(row == k, done, w - low * done)
        for j in range(k + 1, n):
            cols[j] = cols[j] - low * low[j : j + 1, :]
    return w


def gram_kernel(f_ref, o_ref, acc_ref):
    step = pl.program_id(0)

    @pl.when(step == 0)
    def _():
        acc_ref[...] = jnp.zeros_like(acc_ref)

    x = jnp.concatenate(split(f_ref[0], 3), axis=0)
    acc_ref[...] += lax.dot_general(
        x, x, (((1,), (1,)), ((), ())), preferred_element_type=f32
    )

    @pl.when(step == pl.num_programs(0) - 1)
    def _():
        a = acc_ref[...]
        rows = (a[2 * LEV :] + a[LEV : 2 * LEV]) + a[:LEV]
        g = (rows[:, 2 * LEV :] + rows[:, LEV : 2 * LEV]) + rows[:, :LEV]
        h = LEV // 2
        o_ref[...] = jnp.concatenate(
            [g[:h, :], g[h:, h:], jnp.zeros((h, LANES - LEV - h), f32)], axis=1
        )


def level_gram(field, chunk=4096):
    cells = field.shape[2]
    return pl.pallas_call(
        gram_kernel,
        grid=(cells // chunk,),
        in_specs=[pl.BlockSpec((1, LEV, chunk), lambda i: (0, 0, i))],
        out_specs=pl.BlockSpec((LEV // 2, LANES), lambda i: (0, 0)),
        out_shape=jax.ShapeDtypeStruct((LEV // 2, LANES), f32),
        scratch_shapes=[pltpu.VMEM((3 * LEV, 3 * LEV), f32)],
        name="level_gram",
    )(field)


def level_kernel(g_ref, s_ref, basis_ref, lhs_ref):
    h = LEV // 2
    s = g_ref[...]
    lane = lax.broadcasted_iota(jnp.int32, (h, LANES), 1)
    top = jnp.where(lane < LEV, s, 0.0)
    moved = pltpu.roll(s, LANES - h, 1)
    square = jnp.concatenate([moved, jnp.zeros((LANES - h, LANES), f32)], axis=0).T
    bottom = jnp.where(lane < h, square[:h, :], jnp.where(lane < LEV, moved, 0.0))
    gram = jnp.concatenate(
        [top, bottom, jnp.zeros((LANES - LEV, LANES), f32)], axis=0
    )
    v = orth_rows(s_ref[...], R1)
    for _ in range(ITERS):
        w = jnp.dot(v, gram, precision=highest, preferred_element_type=f32)
        v = orth_rows(w, R1)
    wide = jnp.concatenate([v, jnp.zeros((LANES - R1, LANES), f32)], axis=0)
    basis_ref[...] = wide.T[:LEV, :R1]
    v2 = jnp.concatenate([v, jnp.zeros((R1, LANES), f32)], axis=1)
    v3 = v2 + pltpu.roll(v2, LEV, 1) + pltpu.roll(v2, 2 * LEV, 1)
    lhs_ref[...] = jnp.concatenate(
        [p.astype(f32) for p in split(v3, 3)], axis=0
    ).astype(bf16)


def level_factor(gram, start_rows):
    return pl.pallas_call(
        level_kernel,
        out_shape=(
            jax.ShapeDtypeStruct((LEV, R1), f32),
            jax.ShapeDtypeStruct((3 * R1, 2 * LANES), bf16),
        ),
        name="level_factor",
    )(gram, start_rows)


def project_kernel(lhs_ref, f_ref, o_ref, tmp_ref):
    chunk = f_ref.shape[2]
    x = jnp.concatenate(
        split(f_ref[0], 3) + [jnp.zeros((16, chunk), bf16)], axis=0
    )
    p = jnp.dot(lhs_ref[...], x, preferred_element_type=f32)
    r = (p[2 * R1 :] + p[R1 : 2 * R1]) + p[:R1]
    for m in range(chunk // (8 * LANES)):
        for j in range(8):
            at = (m * 8 + j) * LANES
            tmp_ref[m, j * R1 : (j + 1) * R1, :] = r[:, at : at + LANES]
        for d in range(8):
            for k in range(3):
                o_ref[d, k * 8 : (k + 1) * 8, m * LANES : (m + 1) * LANES] = tmp_ref[
                    m, pl.ds(3 * d + k, 8, stride=R1), :
                ]


def project(lhs, field, chunk=4096):
    cells = field.shape[2]
    return pl.pallas_call(
        project_kernel,
        grid=(cells // chunk,),
        in_specs=[
            pl.BlockSpec((3 * R1, 2 * LANES), lambda i: (0, 0)),
            pl.BlockSpec((1, LEV, chunk), lambda i: (0, 0, i)),
        ],
        out_specs=pl.BlockSpec((8, R1, chunk // 8), lambda i: (0, 0, i)),
        out_shape=jax.ShapeDtypeStruct((8, R1, cells // 8), f32),
        scratch_shapes=[pltpu.VMEM((chunk // (8 * LANES), 8 * R1, LANES), f32)],
        name="project",
    )(lhs, field)


PAIRS = [(s, t) for s in range(SNAP) for t in range(s, SNAP)]


def time_gram_kernel(x_ref, o_ref, acc_ref):
    step = pl.program_id(0)

    @pl.when(step == 0)
    def _():
        acc_ref[...] = jnp.zeros_like(acc_ref)

    def body(i, acc):
        at = pl.multiple_of(i * LANES, LANES)
        acc = list(acc)
        for k in range(R1 // 8):
            xs = [x_ref[s, k * 8 : (k + 1) * 8, pl.ds(at, LANES)] for s in range(SNAP)]
            for n, (s, t) in enumerate(PAIRS):
                acc[n] = acc[n] + xs[s] * xs[t]
        return tuple(acc)

    acc = lax.fori_loop(
        0,
        x_ref.shape[2] // LANES,
        body,
        tuple(acc_ref[n] for n in range(len(PAIRS))),
    )
    for n in range(len(PAIRS)):
        acc_ref[n] = acc[n]

    @pl.when(step == pl.num_programs(0) - 1)
    def _():
        row = lax.broadcasted_iota(jnp.int32, (SNAP, LANES), 0)
        lane = lax.broadcasted_iota(jnp.int32, (SNAP, LANES), 1)
        out = jnp.zeros((SNAP, LANES), f32)
        for t in range(SNAP):
            part = jnp.zeros((SNAP, LANES), f32)
            for s in range(SNAP):
                n = PAIRS.index((min(s, t), max(s, t)))
                part = jnp.where(row == s, jnp.sum(acc[n], axis=0, keepdims=True), part)
            out = jnp.where(lane == t, jnp.sum(part, axis=1, keepdims=True), out)
        o_ref[...] = out


def time_gram(x, chunk=1024):
    lanes = x.shape[2]
    return pl.pallas_call(
        time_gram_kernel,
        grid=(lanes // chunk,),
        in_specs=[pl.BlockSpec((SNAP, R1, chunk), lambda i: (0, 0, i))],
        out_specs=pl.BlockSpec((SNAP, LANES), lambda i: (0, 0)),
        out_shape=jax.ShapeDtypeStruct((SNAP, LANES), f32),
        scratch_shapes=[pltpu.VMEM((len(PAIRS), 8, LANES), f32)],
        name="time_gram",
    )(x)


def core_kernel(g_ref, s_ref, x_ref, o_ref, basis_ref, splat_ref, tmp_ref):
    @pl.when(pl.program_id(0) == 0)
    def _():
        g = g_ref[...]
        v = orth_rows(s_ref[...], R2)
        for _ in range(ITERS):
            w = jnp.zeros((8, LANES), f32)
            for s in range(SNAP):
                w = w + v[:, s : s + 1] * g[s : s + 1, :]
            v = orth_rows(w, R2)
        basis_ref[...] = v
        for q in range(R2):
            for s in range(SNAP):
                splat_ref[q, s] = jnp.broadcast_to(v[q : q + 1, s : s + 1], (8, LANES))

    for m in range(x_ref.shape[2] // LANES):
        for k in range(R1 // 8):
            xs = [
                x_ref[s, k * 8 : (k + 1) * 8, m * LANES : (m + 1) * LANES]
                for s in range(SNAP)
            ]
            for q in range(R2):
                c = xs[0] * splat_ref[q, 0]
                for s in range(1, SNAP):
                    c = c + xs[s] * splat_ref[q, s]
                tmp_ref[m, q, k * 8 : (k + 1) * 8, :] = c
        for q in range(R2):
            for j in range(8):
                at = (m * 8 + j) * LANES
                o_ref[q, :, at : at + LANES] = tmp_ref[
                    m, q, pl.ds(j, R1 // 8, stride=8), :
                ]


def time_core(gram, start_rows, x, chunk=512):
    lanes = x.shape[2]
    return pl.pallas_call(
        core_kernel,
        grid=(lanes // chunk,),
        in_specs=[
            pl.BlockSpec((SNAP, LANES), lambda i: (0, 0)),
            pl.BlockSpec((SNAP, LANES), lambda i: (0, 0)),
            pl.BlockSpec((SNAP, R1, chunk), lambda i: (0, 0, i)),
        ],
        out_specs=(
            pl.BlockSpec((R2, R1 // 8, 8 * chunk), lambda i: (0, 0, i)),
            pl.BlockSpec((SNAP, LANES), lambda i: (0, 0)),
        ),
        out_shape=(
            jax.ShapeDtypeStruct((R2, R1 // 8, 8 * lanes), f32),
            jax.ShapeDtypeStruct((SNAP, LANES), f32),
        ),
        scratch_shapes=[
            pltpu.VMEM((R2, SNAP, 8, LANES), f32),
            pltpu.VMEM((chunk // LANES, R2, R1, LANES), f32),
        ],
        name="time_core",
    )(gram, start_rows, x)


def tree(xs):
    while len(xs) > 1:
        xs = [xs[i] + xs[i + 1] for i in range(0, len(xs), 2)]
    return xs[0]


def exchange(x, axis, size, masks):
    return tree(
        [x]
        + [lax.ppermute(x, axis, [(i, i ^ m) for i in range(size)]) for m in masks]
    )


def sum_level(x):
    x = exchange(x, "lt", 8, (1,))
    x = exchange(x, "lt", 8, (2, 4, 6))
    x = exchange(x, "cell", 32, (8, 16, 24))
    x = exchange(x, "cell", 32, (1, 2, 3))
    return exchange(x, "cell", 32, (4,))


def spread(x, axis, size):
    y = jnp.broadcast_to(x[None], (size,) + x.shape)
    y = lax.all_to_all(y, axis, split_axis=0, concat_axis=0, tiled=True)
    return y.sum(0)


def body(field, level_start, time_start):
    level_rows = jnp.pad(level_start.T, ((0, 0), (0, LANES - LEV)))
    time_rows = jnp.pad(time_start.T, ((0, SNAP - R2), (0, LANES - SNAP)))
    gram = sum_level(level_gram(field))
    level_basis, lhs = level_factor(gram, level_rows)
    blocks = project(lhs, field)
    blocks = lax.all_to_all(blocks, "lt", split_axis=0, concat_axis=0, tiled=True)
    tgram = time_gram(blocks)
    tgram = spread(spread(tgram, "lt", 8), "cell", 32)
    core, trows = time_core(tgram, time_rows, blocks)
    return core, level_basis, trows[:R2, :SNAP].T


def solution(mesh):
    placed = (P("lt", None, "cell"), P(), P())
    return jax.shard_map(
        body,
        mesh=mesh,
        in_specs=placed,
        out_specs=(P(None, "lt", "cell"), P(), P()),
        check_vma=False,
    )
```

```python
import jax
import jax.numpy as jnp
from jax import lax
from jax.experimental import pallas as pl
from jax.experimental.pallas import tpu as pltpu
from jax.sharding import PartitionSpec as P

ITERS = 3
highest = lax.Precision.HIGHEST
f32 = jnp.float32
bf16 = jnp.bfloat16
LEV, R1, SNAP, R2 = 80, 24, 8, 6
LANES = 128


def split(x, parts):
    out = []
    for _ in range(parts):
        top = x.astype(bf16)
        out.append(top)
        x = x - top.astype(f32)
    return out


def orth_rows(w, n):
    rows = w.shape[0]
    cols = [
        jnp.broadcast_to(jnp.sum(w * w[k : k + 1, :], axis=1, keepdims=True), w.shape)
        for k in range(n)
    ]
    row = lax.broadcasted_iota(jnp.int32, w.shape, 0)
    for k in range(n):
        pivot = cols[k][k : k + 1, :]
        inv = lax.rsqrt(pivot)
        inv = inv * (1.5 - (0.5 * pivot * inv) * inv)
        done = w[k : k + 1, :] * inv
        low = jnp.where(row > k, cols[k] * inv, 0.0)
        w = jnp.where(row == k, done, w - low * done)
        for j in range(k + 1, n):
            cols[j] = cols[j] - low * low[j : j + 1, :]
    return w


def gram_kernel(f_ref, o_ref, buf_ref, acc_ref, sem):
    count, _, chunk = buf_ref.shape

    def copy(i):
        at = pl.multiple_of(i * chunk, chunk)
        return pltpu.make_async_copy(
            f_ref.at[0, :, pl.ds(at, chunk)], buf_ref.at[i], sem.at[i]
        )

    for i in range(count):
        copy(i).start()
    acc_ref[...] = jnp.zeros_like(acc_ref)

    def step(i, carry):
        copy(i).wait()
        x = jnp.concatenate(split(buf_ref[i], 3), axis=0)
        acc_ref[...] += lax.dot_general(
            x, x, (((1,), (1,)), ((), ())), preferred_element_type=f32
        )
        return carry

    lax.fori_loop(0, count, step, 0)
    a = acc_ref[...]
    rows = (a[2 * LEV :] + a[LEV : 2 * LEV]) + a[:LEV]
    g = (rows[:, 2 * LEV :] + rows[:, LEV : 2 * LEV]) + rows[:, :LEV]
    h = LEV // 2
    o_ref[...] = jnp.concatenate(
        [g[:h, :], g[h:, h:], jnp.zeros((h, LANES - LEV - h), f32)], axis=1
    )


def level_gram(field, chunk=8192):
    cells = field.shape[2]
    count = cells // chunk
    return pl.pallas_call(
        gram_kernel,
        in_specs=[pl.BlockSpec(memory_space=pl.ANY)],
        out_specs=pl.BlockSpec(memory_space=pltpu.VMEM),
        out_shape=jax.ShapeDtypeStruct((LEV // 2, LANES), f32),
        scratch_shapes=[
            pltpu.VMEM((count, LEV, chunk), f32),
            pltpu.VMEM((3 * LEV, 3 * LEV), f32),
            pltpu.SemaphoreType.DMA((count,)),
        ],
        name="level_gram",
    )(field)


def square_of(x):
    r, c = x.shape
    if c < LANES:
        x = jnp.concatenate([x, jnp.zeros((r, LANES - c), f32)], axis=1)
    return jnp.concatenate([x, jnp.zeros((LANES - r, LANES), f32)], axis=0)


def start_kernel(l_ref, t_ref, lo_ref, to_ref):
    lo_ref[...] = orth_rows(square_of(l_ref[...])[:R1, :], R1)
    to_ref[...] = orth_rows(square_of(t_ref[...]).T[:SNAP, :], R2)


def start_factors(level_rows, time_start):
    return pl.pallas_call(
        start_kernel,
        out_shape=(
            jax.ShapeDtypeStruct((R1, LANES), f32),
            jax.ShapeDtypeStruct((SNAP, LANES), f32),
        ),
        cost_estimate=pl.CostEstimate(
            flops=4000000, bytes_accessed=100000, transcendentals=0
        ),
        name="start_factors",
    )(level_rows, time_start)


def level_kernel(g_ref, h_ref, v_ref, basis_ref, lhs_ref):
    h = LEV // 2
    s = g_ref[...] + h_ref[...]
    lane = lax.broadcasted_iota(jnp.int32, (h, LANES), 1)
    top = jnp.where(lane < LEV, s, 0.0)
    moved = pltpu.roll(s, LANES - h, 1)
    square = square_of(moved).T
    bottom = jnp.where(lane < h, square[:h, :], jnp.where(lane < LEV, moved, 0.0))
    gram = jnp.concatenate(
        [top, bottom, jnp.zeros((LANES - LEV, LANES), f32)], axis=0
    )
    v = v_ref[...]
    for _ in range(ITERS):
        w = jnp.dot(v, gram, precision=highest, preferred_element_type=f32)
        v = orth_rows(w, R1)
    basis_ref[...] = v[:, :LEV]
    v2 = jnp.concatenate([v, jnp.zeros((R1, LANES), f32)], axis=1)
    v3 = v2 + pltpu.roll(v2, LEV, 1) + pltpu.roll(v2, 2 * LEV, 1)
    lhs_ref[...] = jnp.concatenate(
        [p.astype(f32) for p in split(v3, 3)], axis=0
    ).astype(bf16)


def level_factor(half, other, start_rows):
    return pl.pallas_call(
        level_kernel,
        out_shape=(
            jax.ShapeDtypeStruct((R1, LEV), f32),
            jax.ShapeDtypeStruct((3 * R1, 2 * LANES), bf16),
        ),
        name="level_factor",
    )(half, other, start_rows)


def project(lhs, field, first, cells, chunk=4096):
    count = cells // chunk
    part = chunk // 8

    def kernel(lhs_ref, f_ref, o_ref, buf_ref, tmp_ref, out_ref, sem, out_sem):
        def copy(i):
            at = pl.multiple_of(first + i * chunk, chunk)
            return pltpu.make_async_copy(
                f_ref.at[0, :, pl.ds(at, chunk)], buf_ref.at[i], sem.at[i]
            )

        def copy_out(i):
            at = pl.multiple_of(i * part, part)
            return pltpu.make_async_copy(
                out_ref.at[i], o_ref.at[:, :, pl.ds(at, part)], out_sem.at[i]
            )

        for i in range(count):
            copy(i).start()

        def step(i, carry):
            copy(i).wait()
            x = jnp.concatenate(
                split(buf_ref[i], 3) + [jnp.zeros((16, chunk), bf16)], axis=0
            )
            p = jnp.dot(lhs_ref[...], x, preferred_element_type=f32)
            r = (p[2 * R1 :] + p[R1 : 2 * R1]) + p[:R1]
            for m in range(chunk // (8 * LANES)):
                for j in range(8):
                    at = (m * 8 + j) * LANES
                    tmp_ref[m, j * R1 : (j + 1) * R1, :] = r[:, at : at + LANES]
                for d in range(8):
                    for k in range(3):
                        out_ref[
                            i, d, k * 8 : (k + 1) * 8, m * LANES : (m + 1) * LANES
                        ] = tmp_ref[m, pl.ds(3 * d + k, 8, stride=R1), :]
            copy_out(i).start()
            return carry

        lax.fori_loop(0, count, step, 0)
        for i in range(count):
            copy_out(i).wait()

    return pl.pallas_call(
        kernel,
        in_specs=[
            pl.BlockSpec(memory_space=pltpu.VMEM),
            pl.BlockSpec(memory_space=pl.ANY),
        ],
        out_specs=pl.BlockSpec(memory_space=pl.ANY),
        out_shape=jax.ShapeDtypeStruct((8, R1, cells // 8), f32),
        scratch_shapes=[
            pltpu.VMEM((count, LEV, chunk), f32),
            pltpu.VMEM((chunk // (8 * LANES), 8 * R1, LANES), f32),
            pltpu.VMEM((count, 8, R1, part), f32),
            pltpu.SemaphoreType.DMA((count,)),
            pltpu.SemaphoreType.DMA((count,)),
        ],
        cost_estimate=pl.CostEstimate(
            flops=8 * LEV * R1 * cells, bytes_accessed=5 * LEV * cells, transcendentals=0
        ),
        name="project",
    )(lhs, field)


PAIRS = [(s, t) for s in range(SNAP) for t in range(s, SNAP)]


def time_gram_kernel(x_ref, o_ref):
    def step(i, acc):
        at = pl.multiple_of(i * LANES, LANES)
        acc = list(acc)
        for k in range(R1 // 8):
            xs = [x_ref[s, k * 8 : (k + 1) * 8, pl.ds(at, LANES)] for s in range(SNAP)]
            for n, (s, t) in enumerate(PAIRS):
                acc[n] = acc[n] + xs[s] * xs[t]
        return tuple(acc)

    acc = lax.fori_loop(
        0,
        x_ref.shape[2] // LANES,
        step,
        tuple(jnp.zeros((8, LANES), f32) for _ in PAIRS),
    )
    row = lax.broadcasted_iota(jnp.int32, (SNAP, LANES), 0)
    lane = lax.broadcasted_iota(jnp.int32, (SNAP, LANES), 1)
    sums = [jnp.sum(a, axis=0, keepdims=True) for a in acc]
    out = jnp.zeros((1, LANES), f32)
    for t in range(SNAP):
        part = jnp.zeros((SNAP, LANES), f32)
        for s in range(SNAP):
            part = jnp.where(row == s, sums[PAIRS.index((min(s, t), max(s, t)))], part)
        total = jnp.sum(part, axis=1, keepdims=True)
        out = out + jnp.sum(
            jnp.where(lane == row * SNAP + t, total, 0.0), axis=0, keepdims=True
        )
    o_ref[...] = jnp.broadcast_to(out[None], o_ref.shape)


def time_gram(x, copies):
    return pl.pallas_call(
        time_gram_kernel,
        out_shape=jax.ShapeDtypeStruct((copies, 1, LANES), f32),
        cost_estimate=pl.CostEstimate(
            flops=72 * R1 * x.shape[2], bytes_accessed=32 * R1 * x.shape[2], transcendentals=0
        ),
        name="time_gram",
    )(x)


def time_core(gram, start_rows, x, parts=4):
    lanes = x.shape[2] // parts

    def kernel(
        g_ref, s_ref, x_ref, o_ref, basis_ref, buf_ref, splat_ref, tmp_ref, out_ref, sem, out_sem
    ):
        def copy(c):
            return pltpu.make_async_copy(
                x_ref.at[:, :, pl.ds(c * lanes, lanes)], buf_ref.at[c], sem.at[c]
            )

        for c in range(parts):
            copy(c).start()
        flat = jnp.broadcast_to(jnp.sum(g_ref[...], axis=0), (SNAP, LANES))
        row = lax.broadcasted_iota(jnp.int32, (SNAP, LANES), 0)
        lane = lax.broadcasted_iota(jnp.int32, (SNAP, LANES), 1)
        g = jnp.zeros((SNAP, LANES), f32)
        for s in range(SNAP):
            moved = pltpu.roll(flat, (LANES - s * SNAP) % LANES, 1) if s else flat
            g = jnp.where((row == s) & (lane < SNAP), moved, g)
        v = s_ref[...]
        for _ in range(ITERS):
            w = jnp.zeros((8, LANES), f32)
            for s in range(SNAP):
                w = w + v[:, s : s + 1] * g[s : s + 1, :]
            v = orth_rows(w, R2)
        for q in range(R2):
            for s in range(SNAP):
                splat_ref[q, s] = jnp.broadcast_to(v[q : q + 1, s : s + 1], (8, LANES))
        basis_ref[...] = square_of(v).T[:SNAP, :R2]

        def copy_out(c):
            return pltpu.make_async_copy(
                out_ref.at[c],
                o_ref.at[:, :, pl.ds(c * 8 * lanes, 8 * lanes)],
                out_sem.at[c],
            )

        for c in range(parts):
            copy(c).wait()

            def step(i, carry):
                for u in range(2):
                    m = i * 2 + u
                    at = pl.multiple_of(m * LANES, LANES)
                    x = [
                        [
                            buf_ref[c, s, k * 8 : (k + 1) * 8, pl.ds(at, LANES)]
                            for s in range(SNAP)
                        ]
                        for k in range(R1 // 8)
                    ]
                    for q in range(R2):
                        acc = [None] * (R1 // 8)
                        for s in range(SNAP):
                            b = splat_ref[q, s]
                            for k in range(R1 // 8):
                                y = x[k][s] * b
                                acc[k] = y if s == 0 else acc[k] + y
                        for k in range(R1 // 8):
                            tmp_ref[u, q, k * 8 : (k + 1) * 8, :] = acc[k]
                    for q in range(R2):
                        for j in range(8):
                            to = pl.multiple_of((m * 8 + j) * LANES, LANES)
                            out_ref[c, q, :, pl.ds(to, LANES)] = tmp_ref[
                                u, q, pl.ds(j, R1 // 8, stride=8), :
                            ]
                return carry

            lax.fori_loop(0, lanes // (2 * LANES), step, 0)
            copy_out(c).start()
        for c in range(parts):
            copy_out(c).wait()

    vmem = pl.BlockSpec(memory_space=pltpu.VMEM)
    hbm = pl.BlockSpec(memory_space=pl.ANY)
    return pl.pallas_call(
        kernel,
        in_specs=[vmem, vmem, hbm],
        out_specs=(hbm, vmem),
        out_shape=(
            jax.ShapeDtypeStruct((R2, R1 // 8, 8 * lanes * parts), f32),
            jax.ShapeDtypeStruct((SNAP, R2), f32),
        ),
        scratch_shapes=[
            pltpu.VMEM((parts, SNAP, R1, lanes), f32),
            pltpu.VMEM((R2, SNAP, 8, LANES), f32),
            pltpu.VMEM((2, R2, R1, LANES), f32),
            pltpu.VMEM((parts, R2, R1 // 8, 8 * lanes), f32),
            pltpu.SemaphoreType.DMA((parts,)),
            pltpu.SemaphoreType.DMA((parts,)),
        ],
        name="time_core",
    )(gram, start_rows, x)


def tree(xs):
    while len(xs) > 1:
        xs = [xs[i] + xs[i + 1] for i in range(0, len(xs), 2)]
    return xs[0]


def exchange(x, axis, size, masks):
    return tree(
        [x]
        + [lax.ppermute(x, axis, [(i, i ^ m) for i in range(size)]) for m in masks]
    )


def on_chip(x):
    return pltpu.with_memory_space_constraint(x, pltpu.VMEM)


def sum_level(x):
    x = exchange(x, "lt", 8, (1,))
    x = exchange(x, "lt", 8, (2, 4, 6))
    x = exchange(x, "cell", 32, (8, 16, 24))
    x = exchange(x, "cell", 32, (1, 2, 3))
    other = lax.ppermute(x, "cell", [(i, i ^ 4) for i in range(32)])
    return on_chip(x), on_chip(other)


def body(field, level_start, time_start):
    both = ("cell", "lt")
    level_rows, time_rows = start_factors(level_start.T, time_start)
    half, other = sum_level(level_gram(field))
    level_rows, lhs = level_factor(half, other, level_rows)
    blocks = project(lhs, field, 0, field.shape[2])
    blocks = lax.all_to_all(blocks, "lt", split_axis=0, concat_axis=0, tiled=True)
    tgram = time_gram(on_chip(blocks), 256)
    tgram = on_chip(
        lax.all_to_all(tgram, both, split_axis=0, concat_axis=0, tiled=True)
    )
    core, time_basis = time_core(tgram, time_rows, blocks)
    return core, level_rows.T, time_basis


def solution(mesh):
    placed = (P("lt", None, "cell"), P(), P())
    return jax.shard_map(
        body,
        mesh=mesh,
        in_specs=placed,
        out_specs=(P(None, "lt", "cell"), P(), P()),
        check_vma=False,
    )
```

```python
import jax
import jax.numpy as jnp
from jax import lax
from jax.experimental import pallas as pl
from jax.experimental.pallas import tpu as pltpu
from jax.sharding import PartitionSpec as P

ITERS = 3
highest = lax.Precision.HIGHEST
f32 = jnp.float32
bf16 = jnp.bfloat16
LEV, R1, SNAP, R2 = 80, 24, 8, 6
LANES = 128


def split(x, parts):
    out = []
    for _ in range(parts):
        top = x.astype(bf16)
        out.append(top)
        x = x - top.astype(f32)
    return out


def orth_rows(w, n):
    rows = w.shape[0]
    cols = [
        jnp.broadcast_to(jnp.sum(w * w[k : k + 1, :], axis=1, keepdims=True), w.shape)
        for k in range(n)
    ]
    row = lax.broadcasted_iota(jnp.int32, w.shape, 0)
    for k in range(n):
        pivot = cols[k][k : k + 1, :]
        inv = lax.rsqrt(pivot)
        inv = inv * (1.5 - (0.5 * pivot * inv) * inv)
        done = w[k : k + 1, :] * inv
        low = jnp.where(row > k, cols[k] * inv, 0.0)
        w = jnp.where(row == k, done, w - low * done)
        for j in range(k + 1, n):
            cols[j] = cols[j] - low * low[j : j + 1, :]
    return w


def gram_kernel(f_ref, o_ref, buf_ref, acc_ref, sem):
    count, _, chunk = buf_ref.shape

    def copy(i):
        at = pl.multiple_of(i * chunk, chunk)
        return pltpu.make_async_copy(
            f_ref.at[0, :, pl.ds(at, chunk)], buf_ref.at[i], sem.at[i]
        )

    for i in range(count):
        copy(i).start()
    acc_ref[...] = jnp.zeros_like(acc_ref)

    def step(i, carry):
        copy(i).wait()
        x = jnp.concatenate(split(buf_ref[i], 3), axis=0)
        acc_ref[...] += lax.dot_general(
            x, x, (((1,), (1,)), ((), ())), preferred_element_type=f32
        )
        return carry

    lax.fori_loop(0, count, step, 0)
    a = acc_ref[...]
    rows = (a[2 * LEV :] + a[LEV : 2 * LEV]) + a[:LEV]
    g = (rows[:, 2 * LEV :] + rows[:, LEV : 2 * LEV]) + rows[:, :LEV]
    h = LEV // 2
    o_ref[...] = jnp.concatenate(
        [g[:h, :], g[h:, h:], jnp.zeros((h, LANES - LEV - h), f32)], axis=1
    )


def level_gram(field, chunk=8192):
    cells = field.shape[2]
    count = cells // chunk
    return pl.pallas_call(
        gram_kernel,
        in_specs=[pl.BlockSpec(memory_space=pl.ANY)],
        out_specs=pl.BlockSpec(memory_space=pltpu.VMEM),
        out_shape=jax.ShapeDtypeStruct((LEV // 2, LANES), f32),
        scratch_shapes=[
            pltpu.VMEM((count, LEV, chunk), f32),
            pltpu.VMEM((3 * LEV, 3 * LEV), f32),
            pltpu.SemaphoreType.DMA((count,)),
        ],
        name="level_gram",
    )(field)


def square_of(x):
    r, c = x.shape
    if c < LANES:
        x = jnp.concatenate([x, jnp.zeros((r, LANES - c), f32)], axis=1)
    return jnp.concatenate([x, jnp.zeros((LANES - r, LANES), f32)], axis=0)


def start_kernel(l_ref, t_ref, lo_ref, to_ref):
    lo_ref[...] = orth_rows(square_of(l_ref[...])[:R1, :], R1)
    to_ref[...] = orth_rows(square_of(t_ref[...]).T[:SNAP, :], R2)


def start_factors(level_rows, time_start):
    return pl.pallas_call(
        start_kernel,
        out_shape=(
            jax.ShapeDtypeStruct((R1, LANES), f32),
            jax.ShapeDtypeStruct((SNAP, LANES), f32),
        ),
        cost_estimate=pl.CostEstimate(
            flops=4000000, bytes_accessed=100000, transcendentals=0
        ),
        name="start_factors",
    )(level_rows, time_start)


def level_kernel(g_ref, v_ref, basis_ref, lhs_ref):
    h = LEV // 2
    s = tree([g_ref[i] for i in range(g_ref.shape[0])])
    lane = lax.broadcasted_iota(jnp.int32, (h, LANES), 1)
    top = jnp.where(lane < LEV, s, 0.0)
    moved = pltpu.roll(s, LANES - h, 1)
    square = square_of(moved).T
    bottom = jnp.where(lane < h, square[:h, :], jnp.where(lane < LEV, moved, 0.0))
    gram = jnp.concatenate(
        [top, bottom, jnp.zeros((LANES - LEV, LANES), f32)], axis=0
    )
    v = v_ref[...]
    for _ in range(ITERS):
        w = jnp.dot(v, gram, precision=highest, preferred_element_type=f32)
        v = orth_rows(w, R1)
    basis_ref[...] = v[:, :LEV]
    v2 = jnp.concatenate([v, jnp.zeros((R1, LANES), f32)], axis=1)
    v3 = v2 + pltpu.roll(v2, LEV, 1) + pltpu.roll(v2, 2 * LEV, 1)
    lhs_ref[...] = jnp.concatenate(
        [p.astype(f32) for p in split(v3, 3)], axis=0
    ).astype(bf16)


def level_factor(gram, start_rows):
    return pl.pallas_call(
        level_kernel,
        out_shape=(
            jax.ShapeDtypeStruct((R1, LEV), f32),
            jax.ShapeDtypeStruct((3 * R1, 2 * LANES), bf16),
        ),
        name="level_factor",
    )(gram, start_rows)


def project(lhs, field, first, cells, chunk=4096):
    count = cells // chunk
    part = chunk // 8

    def kernel(lhs_ref, f_ref, o_ref, buf_ref, tmp_ref, out_ref, sem, out_sem):
        def copy(i):
            at = pl.multiple_of(first + i * chunk, chunk)
            return pltpu.make_async_copy(
                f_ref.at[0, :, pl.ds(at, chunk)], buf_ref.at[i], sem.at[i]
            )

        def copy_out(i):
            at = pl.multiple_of(i * part, part)
            return pltpu.make_async_copy(
                out_ref.at[i], o_ref.at[:, :, pl.ds(at, part)], out_sem.at[i]
            )

        for i in range(count):
            copy(i).start()

        def step(i, carry):
            copy(i).wait()
            x = jnp.concatenate(
                split(buf_ref[i], 3) + [jnp.zeros((16, chunk), bf16)], axis=0
            )
            p = jnp.dot(lhs_ref[...], x, preferred_element_type=f32)
            r = (p[2 * R1 :] + p[R1 : 2 * R1]) + p[:R1]
            for m in range(chunk // (8 * LANES)):
                for j in range(8):
                    at = (m * 8 + j) * LANES
                    tmp_ref[m, j * R1 : (j + 1) * R1, :] = r[:, at : at + LANES]
                for d in range(8):
                    for k in range(3):
                        out_ref[
                            i, d, k * 8 : (k + 1) * 8, m * LANES : (m + 1) * LANES
                        ] = tmp_ref[m, pl.ds(3 * d + k, 8, stride=R1), :]
            copy_out(i).start()
            return carry

        lax.fori_loop(0, count, step, 0)
        for i in range(count):
            copy_out(i).wait()

    return pl.pallas_call(
        kernel,
        in_specs=[
            pl.BlockSpec(memory_space=pltpu.VMEM),
            pl.BlockSpec(memory_space=pl.ANY),
        ],
        out_specs=pl.BlockSpec(memory_space=pl.ANY),
        out_shape=jax.ShapeDtypeStruct((8, R1, cells // 8), f32),
        scratch_shapes=[
            pltpu.VMEM((count, LEV, chunk), f32),
            pltpu.VMEM((chunk // (8 * LANES), 8 * R1, LANES), f32),
            pltpu.VMEM((count, 8, R1, part), f32),
            pltpu.SemaphoreType.DMA((count,)),
            pltpu.SemaphoreType.DMA((count,)),
        ],
        cost_estimate=pl.CostEstimate(
            flops=8 * LEV * R1 * cells, bytes_accessed=5 * LEV * cells, transcendentals=0
        ),
        name="project",
    )(lhs, field)


PAIRS = [(s, t) for s in range(SNAP) for t in range(s, SNAP)]


def time_gram_kernel(x_ref, o_ref):
    def step(i, acc):
        at = pl.multiple_of(i * LANES, LANES)
        acc = list(acc)
        for k in range(R1 // 8):
            xs = [x_ref[s, k * 8 : (k + 1) * 8, pl.ds(at, LANES)] for s in range(SNAP)]
            for n, (s, t) in enumerate(PAIRS):
                acc[n] = acc[n] + xs[s] * xs[t]
        return tuple(acc)

    acc = lax.fori_loop(
        0,
        x_ref.shape[2] // LANES,
        step,
        tuple(jnp.zeros((8, LANES), f32) for _ in PAIRS),
    )
    row = lax.broadcasted_iota(jnp.int32, (SNAP, LANES), 0)
    lane = lax.broadcasted_iota(jnp.int32, (SNAP, LANES), 1)
    sums = [jnp.sum(a, axis=0, keepdims=True) for a in acc]
    out = jnp.zeros((1, LANES), f32)
    for t in range(SNAP):
        part = jnp.zeros((SNAP, LANES), f32)
        for s in range(SNAP):
            part = jnp.where(row == s, sums[PAIRS.index((min(s, t), max(s, t)))], part)
        total = jnp.sum(part, axis=1, keepdims=True)
        out = out + jnp.sum(
            jnp.where(lane == row * SNAP + t, total, 0.0), axis=0, keepdims=True
        )
    o_ref[...] = jnp.broadcast_to(out[None], o_ref.shape)


def time_gram(x, copies):
    return pl.pallas_call(
        time_gram_kernel,
        out_shape=jax.ShapeDtypeStruct((copies, 1, LANES), f32),
        cost_estimate=pl.CostEstimate(
            flops=72 * R1 * x.shape[2], bytes_accessed=32 * R1 * x.shape[2], transcendentals=0
        ),
        name="time_gram",
    )(x)


def time_core(gram, start_rows, x, parts=4):
    lanes = x.shape[2] // parts

    def kernel(
        g_ref, s_ref, x_ref, o_ref, basis_ref, buf_ref, splat_ref, tmp_ref, out_ref, sem, out_sem
    ):
        def copy(c):
            return pltpu.make_async_copy(
                x_ref.at[:, :, pl.ds(c * lanes, lanes)], buf_ref.at[c], sem.at[c]
            )

        for c in range(parts):
            copy(c).start()
        flat = jnp.broadcast_to(jnp.sum(g_ref[...], axis=0), (SNAP, LANES))
        row = lax.broadcasted_iota(jnp.int32, (SNAP, LANES), 0)
        lane = lax.broadcasted_iota(jnp.int32, (SNAP, LANES), 1)
        g = jnp.zeros((SNAP, LANES), f32)
        for s in range(SNAP):
            moved = pltpu.roll(flat, (LANES - s * SNAP) % LANES, 1) if s else flat
            g = jnp.where((row == s) & (lane < SNAP), moved, g)
        v = s_ref[...]
        for _ in range(ITERS):
            w = jnp.zeros((8, LANES), f32)
            for s in range(SNAP):
                w = w + v[:, s : s + 1] * g[s : s + 1, :]
            v = orth_rows(w, R2)
        for q in range(R2):
            for s in range(SNAP):
                splat_ref[q, s] = jnp.broadcast_to(v[q : q + 1, s : s + 1], (8, LANES))
        basis_ref[...] = square_of(v).T[:SNAP, :R2]

        def copy_out(c):
            return pltpu.make_async_copy(
                out_ref.at[c],
                o_ref.at[:, :, pl.ds(c * 8 * lanes, 8 * lanes)],
                out_sem.at[c],
            )

        for c in range(parts):
            copy(c).wait()

            def step(i, carry):
                for u in range(2):
                    m = i * 2 + u
                    at = pl.multiple_of(m * LANES, LANES)
                    x = [
                        [
                            buf_ref[c, s, k * 8 : (k + 1) * 8, pl.ds(at, LANES)]
                            for s in range(SNAP)
                        ]
                        for k in range(R1 // 8)
                    ]
                    for q in range(R2):
                        acc = [None] * (R1 // 8)
                        for s in range(SNAP):
                            b = splat_ref[q, s]
                            for k in range(R1 // 8):
                                y = x[k][s] * b
                                acc[k] = y if s == 0 else acc[k] + y
                        for k in range(R1 // 8):
                            tmp_ref[u, q, k * 8 : (k + 1) * 8, :] = acc[k]
                    for q in range(R2):
                        for j in range(8):
                            to = pl.multiple_of((m * 8 + j) * LANES, LANES)
                            out_ref[c, q, :, pl.ds(to, LANES)] = tmp_ref[
                                u, q, pl.ds(j, R1 // 8, stride=8), :
                            ]
                return carry

            lax.fori_loop(0, lanes // (2 * LANES), step, 0)
            copy_out(c).start()
        for c in range(parts):
            copy_out(c).wait()

    vmem = pl.BlockSpec(memory_space=pltpu.VMEM)
    hbm = pl.BlockSpec(memory_space=pl.ANY)
    return pl.pallas_call(
        kernel,
        in_specs=[vmem, vmem, hbm],
        out_specs=(hbm, vmem),
        out_shape=(
            jax.ShapeDtypeStruct((R2, R1 // 8, 8 * lanes * parts), f32),
            jax.ShapeDtypeStruct((SNAP, R2), f32),
        ),
        scratch_shapes=[
            pltpu.VMEM((parts, SNAP, R1, lanes), f32),
            pltpu.VMEM((R2, SNAP, 8, LANES), f32),
            pltpu.VMEM((2, R2, R1, LANES), f32),
            pltpu.VMEM((parts, R2, R1 // 8, 8 * lanes), f32),
            pltpu.SemaphoreType.DMA((parts,)),
            pltpu.SemaphoreType.DMA((parts,)),
        ],
        name="time_core",
    )(gram, start_rows, x)


def tree(xs):
    while len(xs) > 1:
        xs = [xs[i] + xs[i + 1] for i in range(0, len(xs), 2)]
    return xs[0]


def exchange(x, axis, size, masks):
    return tree(
        [x]
        + [lax.ppermute(x, axis, [(i, i ^ m) for i in range(size)]) for m in masks]
    )


def on_chip(x):
    return pltpu.with_memory_space_constraint(x, pltpu.VMEM)


def sum_level(x):
    x = exchange(x, "lt", 8, (1,))
    x = exchange(x, "lt", 8, (2, 4, 6))
    x = exchange(x, "cell", 32, (8, 16, 24))
    lines = [[8 * y + z for z in range(8)] for y in range(4)]
    x = jnp.broadcast_to(x[None], (8,) + x.shape)
    return on_chip(
        lax.all_to_all(
            x, "cell", split_axis=0, concat_axis=0, axis_index_groups=lines, tiled=True
        )
    )


def body(field, level_start, time_start):
    both = ("cell", "lt")
    level_rows, time_rows = start_factors(level_start.T, time_start)
    gram = sum_level(level_gram(field))
    level_rows, lhs = level_factor(gram, level_rows)
    blocks = project(lhs, field, 0, field.shape[2])
    blocks = lax.all_to_all(blocks, "lt", split_axis=0, concat_axis=0, tiled=True)
    tgram = time_gram(on_chip(blocks), 256)
    tgram = on_chip(
        lax.all_to_all(tgram, both, split_axis=0, concat_axis=0, tiled=True)
    )
    core, time_basis = time_core(tgram, time_rows, blocks)
    return core, level_rows.T, time_basis


def solution(mesh):
    placed = (P("lt", None, "cell"), P(), P())
    return jax.shard_map(
        body,
        mesh=mesh,
        in_specs=placed,
        out_specs=(P(None, "lt", "cell"), P(), P()),
        check_vma=False,
    )
```

```python
import jax
import jax.numpy as jnp
from jax import lax
from jax.experimental import pallas as pl
from jax.experimental.pallas import tpu as pltpu
from jax.sharding import PartitionSpec as P

ITERS = 3
highest = lax.Precision.HIGHEST
f32 = jnp.float32
bf16 = jnp.bfloat16
LEV, R1, SNAP, R2 = 80, 24, 8, 6
LANES = 128


def split(x, parts):
    out = []
    for _ in range(parts):
        top = x.astype(bf16)
        out.append(top)
        x = x - top.astype(f32)
    return out


def orth_rows(w, n):
    rows = w.shape[0]
    cols = [
        jnp.broadcast_to(jnp.sum(w * w[k : k + 1, :], axis=1, keepdims=True), w.shape)
        for k in range(n)
    ]
    row = lax.broadcasted_iota(jnp.int32, w.shape, 0)
    for k in range(n):
        pivot = cols[k][k : k + 1, :]
        inv = lax.rsqrt(pivot)
        inv = inv * (1.5 - (0.5 * pivot * inv) * inv)
        done = w[k : k + 1, :] * inv
        low = jnp.where(row > k, cols[k] * inv, 0.0)
        w = jnp.where(row == k, done, w - low * done)
        for j in range(k + 1, n):
            cols[j] = cols[j] - low * low[j : j + 1, :]
    return w


def gram_kernel(f_ref, o_ref, buf_ref, acc_ref, sem):
    count, _, chunk = buf_ref.shape

    def copy(i):
        at = pl.multiple_of(i * chunk, chunk)
        return pltpu.make_async_copy(
            f_ref.at[0, :, pl.ds(at, chunk)], buf_ref.at[i], sem.at[i]
        )

    for i in range(count):
        copy(i).start()
    acc_ref[...] = jnp.zeros_like(acc_ref)

    def step(i, carry):
        copy(i).wait()
        x = jnp.concatenate(split(buf_ref[i], 3), axis=0)
        acc_ref[...] += lax.dot_general(
            x, x, (((1,), (1,)), ((), ())), preferred_element_type=f32
        )
        return carry

    lax.fori_loop(0, count, step, 0)
    a = acc_ref[...]
    rows = (a[2 * LEV :] + a[LEV : 2 * LEV]) + a[:LEV]
    g = (rows[:, 2 * LEV :] + rows[:, LEV : 2 * LEV]) + rows[:, :LEV]
    h = LEV // 2
    o_ref[...] = jnp.concatenate(
        [g[:h, :], g[h:, h:], jnp.zeros((h, LANES - LEV - h), f32)], axis=1
    )


def level_gram(field, chunk=8192):
    cells = field.shape[2]
    count = cells // chunk
    return pl.pallas_call(
        gram_kernel,
        in_specs=[pl.BlockSpec(memory_space=pl.ANY)],
        out_specs=pl.BlockSpec(memory_space=pltpu.VMEM),
        out_shape=jax.ShapeDtypeStruct((LEV // 2, LANES), f32),
        scratch_shapes=[
            pltpu.VMEM((count, LEV, chunk), f32),
            pltpu.VMEM((3 * LEV, 3 * LEV), f32),
            pltpu.SemaphoreType.DMA((count,)),
        ],
        name="level_gram",
    )(field)


def square_of(x):
    r, c = x.shape
    if c < LANES:
        x = jnp.concatenate([x, jnp.zeros((r, LANES - c), f32)], axis=1)
    return jnp.concatenate([x, jnp.zeros((LANES - r, LANES), f32)], axis=0)


def start_kernel(l_ref, t_ref, lo_ref, to_ref):
    lo_ref[...] = orth_rows(square_of(l_ref[...])[:R1, :], R1)
    to_ref[...] = orth_rows(square_of(t_ref[...]).T[:SNAP, :], R2)


def start_factors(level_rows, time_start):
    return pl.pallas_call(
        start_kernel,
        out_shape=(
            jax.ShapeDtypeStruct((R1, LANES), f32),
            jax.ShapeDtypeStruct((SNAP, LANES), f32),
        ),
        cost_estimate=pl.CostEstimate(
            flops=4000000, bytes_accessed=100000, transcendentals=0
        ),
        name="start_factors",
    )(level_rows, time_start)


def level_kernel(g_ref, v_ref, basis_ref, lhs_ref):
    h = LEV // 2
    s = tree([g_ref[i] for i in range(g_ref.shape[0])])
    lane = lax.broadcasted_iota(jnp.int32, (h, LANES), 1)
    top = jnp.where(lane < LEV, s, 0.0)
    moved = pltpu.roll(s, LANES - h, 1)
    square = square_of(moved).T
    bottom = jnp.where(lane < h, square[:h, :], jnp.where(lane < LEV, moved, 0.0))
    gram = jnp.concatenate(
        [top, bottom, jnp.zeros((LANES - LEV, LANES), f32)], axis=0
    )
    v = v_ref[...]
    for _ in range(ITERS):
        w = jnp.dot(v, gram, precision=highest, preferred_element_type=f32)
        v = orth_rows(w, R1)
    basis_ref[...] = v[:, :LEV]
    v2 = jnp.concatenate([v, jnp.zeros((R1, LANES), f32)], axis=1)
    v3 = v2 + pltpu.roll(v2, LEV, 1) + pltpu.roll(v2, 2 * LEV, 1)
    lhs_ref[...] = jnp.concatenate(
        [p.astype(f32) for p in split(v3, 3)], axis=0
    ).astype(bf16)


def level_factor(gram, start_rows):
    return pl.pallas_call(
        level_kernel,
        out_shape=(
            jax.ShapeDtypeStruct((R1, LEV), f32),
            jax.ShapeDtypeStruct((3 * R1, 2 * LANES), bf16),
        ),
        name="level_factor",
    )(gram, start_rows)


def project(lhs, field, first, cells, chunk=4096):
    count = cells // chunk
    part = chunk // 8

    def kernel(lhs_ref, f_ref, o_ref, buf_ref, tmp_ref, out_ref, sem, out_sem):
        def copy(i):
            at = pl.multiple_of(first + i * chunk, chunk)
            return pltpu.make_async_copy(
                f_ref.at[0, :, pl.ds(at, chunk)], buf_ref.at[i], sem.at[i]
            )

        def copy_out(i):
            at = pl.multiple_of(i * part, part)
            return pltpu.make_async_copy(
                out_ref.at[i], o_ref.at[:, :, pl.ds(at, part)], out_sem.at[i]
            )

        for i in range(count):
            copy(i).start()

        def step(i, carry):
            copy(i).wait()
            x = jnp.concatenate(
                split(buf_ref[i], 3) + [jnp.zeros((16, chunk), bf16)], axis=0
            )
            p = jnp.dot(lhs_ref[...], x, preferred_element_type=f32)
            r = (p[2 * R1 :] + p[R1 : 2 * R1]) + p[:R1]
            for m in range(chunk // (8 * LANES)):
                for j in range(8):
                    at = (m * 8 + j) * LANES
                    tmp_ref[m, j * R1 : (j + 1) * R1, :] = r[:, at : at + LANES]
                for d in range(8):
                    for k in range(3):
                        out_ref[
                            i, d, k * 8 : (k + 1) * 8, m * LANES : (m + 1) * LANES
                        ] = tmp_ref[m, pl.ds(3 * d + k, 8, stride=R1), :]
            copy_out(i).start()
            return carry

        lax.fori_loop(0, count, step, 0)
        for i in range(count):
            copy_out(i).wait()

    return pl.pallas_call(
        kernel,
        in_specs=[
            pl.BlockSpec(memory_space=pltpu.VMEM),
            pl.BlockSpec(memory_space=pl.ANY),
        ],
        out_specs=pl.BlockSpec(memory_space=pl.ANY),
        out_shape=jax.ShapeDtypeStruct((8, R1, cells // 8), f32),
        scratch_shapes=[
            pltpu.VMEM((count, LEV, chunk), f32),
            pltpu.VMEM((chunk // (8 * LANES), 8 * R1, LANES), f32),
            pltpu.VMEM((count, 8, R1, part), f32),
            pltpu.SemaphoreType.DMA((count,)),
            pltpu.SemaphoreType.DMA((count,)),
        ],
        cost_estimate=pl.CostEstimate(
            flops=8 * LEV * R1 * cells, bytes_accessed=5 * LEV * cells, transcendentals=0
        ),
        name="project",
    )(lhs, field)


PAIRS = [(s, t) for s in range(SNAP) for t in range(s, SNAP)]


def time_gram_kernel(x_ref, o_ref):
    def step(i, acc):
        at = pl.multiple_of(i * LANES, LANES)
        acc = list(acc)
        for k in range(R1 // 8):
            xs = [x_ref[s, k * 8 : (k + 1) * 8, pl.ds(at, LANES)] for s in range(SNAP)]
            for n, (s, t) in enumerate(PAIRS):
                acc[n] = acc[n] + xs[s] * xs[t]
        return tuple(acc)

    acc = lax.fori_loop(
        0,
        x_ref.shape[2] // LANES,
        step,
        tuple(jnp.zeros((8, LANES), f32) for _ in PAIRS),
    )
    row = lax.broadcasted_iota(jnp.int32, (SNAP, LANES), 0)
    lane = lax.broadcasted_iota(jnp.int32, (SNAP, LANES), 1)
    sums = [jnp.sum(a, axis=0, keepdims=True) for a in acc]
    out = jnp.zeros((1, LANES), f32)
    for t in range(SNAP):
        part = jnp.zeros((SNAP, LANES), f32)
        for s in range(SNAP):
            part = jnp.where(row == s, sums[PAIRS.index((min(s, t), max(s, t)))], part)
        total = jnp.sum(part, axis=1, keepdims=True)
        out = out + jnp.sum(
            jnp.where(lane == row * SNAP + t, total, 0.0), axis=0, keepdims=True
        )
    o_ref[...] = jnp.broadcast_to(out[None], o_ref.shape)


def time_gram(x, copies):
    return pl.pallas_call(
        time_gram_kernel,
        out_shape=jax.ShapeDtypeStruct((copies, 1, LANES), f32),
        cost_estimate=pl.CostEstimate(
            flops=72 * R1 * x.shape[2], bytes_accessed=32 * R1 * x.shape[2], transcendentals=0
        ),
        name="time_gram",
    )(x)


def time_core(gram, start_rows, x, parts=8):
    lanes = x.shape[2] // parts

    def kernel(
        g_ref, s_ref, x_ref, o_ref, basis_ref, buf_ref, splat_ref, tmp_ref, out_ref, sem, out_sem
    ):
        def copy(c):
            return pltpu.make_async_copy(
                x_ref.at[:, :, pl.ds(c * lanes, lanes)], buf_ref.at[c], sem.at[c]
            )

        for c in range(parts):
            copy(c).start()
        flat = jnp.broadcast_to(jnp.sum(g_ref[...], axis=0), (SNAP, LANES))
        row = lax.broadcasted_iota(jnp.int32, (SNAP, LANES), 0)
        lane = lax.broadcasted_iota(jnp.int32, (SNAP, LANES), 1)
        g = jnp.zeros((SNAP, LANES), f32)
        for s in range(SNAP):
            moved = pltpu.roll(flat, (LANES - s * SNAP) % LANES, 1) if s else flat
            g = jnp.where((row == s) & (lane < SNAP), moved, g)
        v = s_ref[...]
        for _ in range(ITERS):
            w = jnp.zeros((8, LANES), f32)
            for s in range(SNAP):
                w = w + v[:, s : s + 1] * g[s : s + 1, :]
            v = orth_rows(w, R2)
        for q in range(R2):
            for s in range(SNAP):
                splat_ref[q, s] = jnp.broadcast_to(v[q : q + 1, s : s + 1], (8, LANES))
        basis_ref[...] = square_of(v).T[:SNAP, :R2]

        def copy_out(c):
            return pltpu.make_async_copy(
                out_ref.at[c],
                o_ref.at[:, :, pl.ds(c * 8 * lanes, 8 * lanes)],
                out_sem.at[c],
            )

        for c in range(parts):
            copy(c).wait()

            def step(i, carry):
                for u in range(2):
                    m = i * 2 + u
                    at = pl.multiple_of(m * LANES, LANES)
                    x = [
                        [
                            buf_ref[c, s, k * 8 : (k + 1) * 8, pl.ds(at, LANES)]
                            for s in range(SNAP)
                        ]
                        for k in range(R1 // 8)
                    ]
                    for q in range(R2):
                        acc = [None] * (R1 // 8)
                        for s in range(SNAP):
                            b = splat_ref[q, s]
                            for k in range(R1 // 8):
                                y = x[k][s] * b
                                acc[k] = y if s == 0 else acc[k] + y
                        for k in range(R1 // 8):
                            tmp_ref[u, q, k * 8 : (k + 1) * 8, :] = acc[k]
                    for q in range(R2):
                        for j in range(8):
                            to = pl.multiple_of((m * 8 + j) * LANES, LANES)
                            out_ref[c, q, :, pl.ds(to, LANES)] = tmp_ref[
                                u, q, pl.ds(j, R1 // 8, stride=8), :
                            ]
                return carry

            lax.fori_loop(0, lanes // (2 * LANES), step, 0)
            copy_out(c).start()
        for c in range(parts):
            copy_out(c).wait()

    vmem = pl.BlockSpec(memory_space=pltpu.VMEM)
    hbm = pl.BlockSpec(memory_space=pl.ANY)
    return pl.pallas_call(
        kernel,
        in_specs=[vmem, vmem, hbm],
        out_specs=(hbm, vmem),
        out_shape=(
            jax.ShapeDtypeStruct((R2, R1 // 8, 8 * lanes * parts), f32),
            jax.ShapeDtypeStruct((SNAP, R2), f32),
        ),
        scratch_shapes=[
            pltpu.VMEM((parts, SNAP, R1, lanes), f32),
            pltpu.VMEM((R2, SNAP, 8, LANES), f32),
            pltpu.VMEM((2, R2, R1, LANES), f32),
            pltpu.VMEM((parts, R2, R1 // 8, 8 * lanes), f32),
            pltpu.SemaphoreType.DMA((parts,)),
            pltpu.SemaphoreType.DMA((parts,)),
        ],
        name="time_core",
    )(gram, start_rows, x)


def tree(xs):
    while len(xs) > 1:
        xs = [xs[i] + xs[i + 1] for i in range(0, len(xs), 2)]
    return xs[0]


def exchange(x, axis, size, masks):
    return tree(
        [x]
        + [lax.ppermute(x, axis, [(i, i ^ m) for i in range(size)]) for m in masks]
    )


def on_chip(x):
    return pltpu.with_memory_space_constraint(x, pltpu.VMEM)


def sum_level(x):
    x = exchange(x, "lt", 8, (1,))
    x = exchange(x, "lt", 8, (2, 4, 6))
    x = exchange(x, "cell", 32, (8, 16, 24))
    lines = [[8 * y + z for z in range(8)] for y in range(4)]
    x = jnp.broadcast_to(x[None], (8,) + x.shape)
    return on_chip(
        lax.all_to_all(
            x, "cell", split_axis=0, concat_axis=0, axis_index_groups=lines, tiled=True
        )
    )


def body(field, level_start, time_start):
    both = ("cell", "lt")
    level_rows, time_rows = start_factors(level_start.T, time_start)
    gram = sum_level(level_gram(field))
    level_rows, lhs = level_factor(gram, level_rows)
    blocks = project(lhs, field, 0, field.shape[2])
    blocks = lax.all_to_all(blocks, "lt", split_axis=0, concat_axis=0, tiled=True)
    tgram = time_gram(on_chip(blocks), 256)
    tgram = on_chip(
        lax.all_to_all(tgram, both, split_axis=0, concat_axis=0, tiled=True)
    )
    core, time_basis = time_core(tgram, time_rows, blocks)
    return core, level_rows.T, time_basis


def solution(mesh):
    placed = (P("lt", None, "cell"), P(), P())
    return jax.shard_map(
        body,
        mesh=mesh,
        in_specs=placed,
        out_specs=(P(None, "lt", "cell"), P(), P()),
        check_vma=False,
    )
```
